32 devices in a mesh: groups: 2 (over y), ctx: 8 (over z, x), head: 2 (over core).
Axes of the slice: x: 2, y: 2, z: 4, core: 2. Of those that a mesh axis runs over, the one named last changes fastest.
Arguments:
- attn_query: bfloat16 [2048, 2560], P(('groups', 'ctx'), 'head'), parts along dimension 0, may hold values from -6 to 6
- attn_key: bfloat16 [2048, 2560], P(('groups', 'ctx'), 'head'), parts along dimension 0, may hold values from -6 to 6
- attn_value: bfloat16 [2048, 2560], P(('groups', 'ctx'), 'head'), parts along dimension 0, may hold values from -6 to 6
- lookback: int32 [2048], P(('groups', 'ctx')), parts along dimension 0, may hold values from 192 to 768
- frame_start: int32 [2048], P(('groups', 'ctx')), parts along dimension 0, may hold values from 0 to 1016, as said below
- fast_query: bfloat16 [2048, 2048], P(('groups', 'ctx'), 'head'), parts along dimension 0, may hold values from -6 to 6
- fast_key: bfloat16 [2048, 2048], P(('groups', 'ctx'), 'head'), parts along dimension 0, may hold values from -6 to 6
- fast_value: bfloat16 [2048, 2048], P(('groups', 'ctx'), 'head'), parts along dimension 0, may hold values from -6 to 6
- token_rate: float32 [2048, 4], P(('groups', 'ctx'), 'head'), parts along dimension 0, may hold values from 0.1 to 1
- w_in: float32 [4, 640, 512], P('head', None, 'ctx'), may hold values from -0.25 to 0.25
- w_out: float32 [4, 320, 512], P('head', None, 'ctx'), may hold values from -0.3125 to 0.3125
- momentum_in: float32 [8, 640, 512], P(('groups', 'head'), None, 'ctx'), parts along dimension 0, may hold values from -8 to 8
- momentum_out: float32 [8, 320, 512], P(('groups', 'head'), None, 'ctx'), parts along dimension 0, may hold values from -8 to 8
- step_size: float32 [4], P('head'), may hold values from 0.02 to 0.06
Outputs:
- attn_out: bfloat16 [2048, 2560], P(('groups', 'ctx'), 'head'), parts along dimension 0
- fast_out: bfloat16 [2048, 2048], P(('groups', 'ctx'), 'head'), parts along dimension 0
- new_w_in: float32 [8, 640, 512], P(('groups', 'head'), None, 'ctx'), parts along dimension 0
- new_w_out: float32 [8, 320, 512], P(('groups', 'head'), None, 'ctx'), parts along dimension 0
- new_momentum_in: float32 [8, 640, 512], P(('groups', 'head'), None, 'ctx'), parts along dimension 0
- new_momentum_out: float32 [8, 320, 512], P(('groups', 'head'), None, 'ctx'), parts along dimension 0
The draws below stay inside these ranges and needn't reach their ends.
There are 2 independent parts, one for each index of `groups`. The reference program is written for one: setup_inputs(seed, part) draws one part's arguments, and reference() takes and returns one part's arrays. A program takes and returns all parts, laid end to end along the dimension named above; an argument that names none is the same for every part. Nothing has to cross between parts.
Inputs may be any that keep to these rules, and one draw needn't show every extreme that they name: frame_start never falls along the sequence, is 0 within the first frame, and every frame is a whole multiple of 4 positions long.
All inputs are finite; a program needn't handle non-finite values.
Results may differ from the reference program's by a relative error of at most 0.0095.
Values may be sent and summed in bfloat16 or wider, within the bound.
No kernel may reach another device: no remote copies, remote signals or barrier semaphores. Data moves between devices by JAX's collectives and lax.ppermute only.
A program may use at most 128 MiB of HBM per device.

```python
import math
import jax
import jax.numpy as jnp
from jax import lax

TOK_DEV = 128
ATT_HEADS = 20
ATT_DIM = 128
HEADS = 4
DH = 512
FH = 320
WINDOW = 768
FRAME_SPAN = 256
TOKENS = 1024


def attn_pair(key):
    col_count = ATT_HEADS * ATT_DIM
    key_query, key_keys = jax.random.split(jax.random.fold_in(key, 71), 2)
    query_vals = jnp.clip(jax.random.normal(key_query, (TOKENS, col_count), jnp.float32), -6.0, 6.0)
    key_vals = jnp.clip(jax.random.normal(key_keys, (TOKENS, col_count), jnp.float32), -6.0, 6.0)
    return (query_vals, key_vals)


def draw_attn_query(key, part):
    return attn_pair(key)[0].astype(jnp.bfloat16)


def draw_attn_key(key, part):
    return attn_pair(key)[1].astype(jnp.bfloat16)


def draw_frame_start(key, part):
    positions = jnp.arange(TOKENS, dtype=jnp.int32)
    picked = jax.random.randint(jax.random.fold_in(key, 13), (TOKENS,), 0, FRAME_SPAN // 4)
    opening = (positions % 4 == 0) & (picked == 0) | (positions == 0)
    opening = opening | (positions == TOKENS - 4) | (positions == TOKENS - 8)
    own_first = lax.cummax(jnp.where(opening, positions, 0), axis=0)
    before = jnp.maximum(own_first - 1, 0)
    return jnp.take(own_first, before).astype(jnp.int32)


def state_draw(key, row_count):
    key_base, key_rows, key_cols = jax.random.split(jax.random.fold_in(key, 29), 3)
    arr_shape = (HEADS, row_count, DH)
    base_vals = jnp.clip(jax.random.normal(key_base, arr_shape, jnp.float32), -4.0, 4.0)
    row_scale = jnp.exp(jax.random.uniform(key_rows, (HEADS, row_count, 1), jnp.float32, 0.0, math.log(10.0)))
    col_scale = jnp.exp(jax.random.uniform(key_cols, (1, 1, DH), jnp.float32, 0.0, math.log(10.0)))
    return 0.02 * base_vals * row_scale * col_scale


def draw_momentum_in(key, part):
    return state_draw(key, 2 * FH)


def draw_momentum_out(key, part):
    return state_draw(key, FH)


def with_ends(drawn, own_key, low, top_value):
    longest = drawn.shape.index(max(drawn.shape))
    spots = []
    for shift in (0, 1):
        where = [jax.random.randint(jax.random.fold_in(own_key, axis), (), 0, length) for axis, length in enumerate(drawn.shape)]
        where[longest] = (where[longest] + shift) % drawn.shape[longest]
        spots.append(tuple(where))
    return drawn.at[spots[0]].set(low).at[spots[1]].set(top_value)


def with_spikes(drawn, stream_key, source, target, blocks, factor):
    def block_of(dim):
        return (jnp.arange(drawn.shape[dim]) // (drawn.shape[dim] // blocks)).reshape((-1,) + (1,) * (drawn.ndim - 1 - dim))

    one_side = jax.random.permutation(stream_key, blocks)[block_of(target)]
    other_side = (block_of(target) + blocks // 2) % blocks
    return jnp.where((block_of(source) == one_side) | (block_of(source) == other_side), factor * drawn, drawn)


def block_levels(own_key, dims, cuts, smallest, top_value):
    level, own = 1.0, jax.random.fold_in(own_key, 6)
    for position, parts in cuts:
        draws = jnp.exp(jax.random.uniform(jax.random.fold_in(own, position), (parts,), jnp.float32, smallest / len(cuts), top_value / len(cuts)))
        level = level * jnp.repeat(draws, dims[position] // parts).reshape([-1 if axis == position else 1 for axis in range(len(dims))])
    return level


def gaussian(own_key, shape, spread, most, cuts=(), kind=jnp.bfloat16):
    drawn = jax.random.normal(own_key, shape, jnp.float32) * spread
    if len(cuts) > 0:
        drawn = block_levels(own_key, shape, cuts, -0.22, 0.18) * drawn
    return jnp.clip(drawn, min=-most, max=most).astype(kind)


def bell_draw_with(key, extent, width, most, shards, heavy, held_as=jnp.bfloat16):
    array = width * jax.random.normal(key, extent, jnp.float32)
    if shards:
        array = array * block_levels(key, extent, shards, -0.22, 0.18)
    return jnp.clip(with_spikes(array, jax.random.fold_in(key, 3), *heavy), -most, most).astype(held_as)


def setup_inputs(seed: int = 0, part: int = 0) -> dict:
    seeds = jax.random.split(jax.random.key(seed), 15)
    part_splits = jax.random.split(jax.random.fold_in(seeds[14], part), 15)
    return {
        "attn_query": draw_attn_query(jax.random.fold_in(jax.random.fold_in(seeds[14], part), 71), part),
        "attn_key": draw_attn_key(jax.random.fold_in(jax.random.fold_in(seeds[14], part), 71), part),
        "attn_value": gaussian(part_splits[2], (TOKENS, ATT_HEADS * ATT_DIM), 1.0, 6.0, ((0, 8), (1, 2))),
        "lookback": with_ends(jax.random.randint(part_splits[3], (TOKENS,), WINDOW // 4, WINDOW + 1), jax.random.fold_in(part_splits[3], 1), WINDOW // 4, WINDOW).astype(jnp.int32),
        "frame_start": draw_frame_start(jax.random.fold_in(jax.random.fold_in(seeds[14], part), 71), part),
        "fast_query": gaussian(part_splits[5], (TOKENS, HEADS * DH), 1.0, 6.0, ((0, 8), (1, 2))),
        "fast_key": gaussian(part_splits[6], (TOKENS, HEADS * DH), 1.0, 6.0, ((0, 8), (1, 2))),
        "fast_value": bell_draw_with(part_splits[7], (TOKENS, HEADS * DH), 1.0, 6.0, ((0, 8), (1, 2)), (0, 1, 8, 2.0)),
        "token_rate": jnp.clip(jnp.exp(math.log(1.0) - 2.3025851 * jax.random.uniform(part_splits[8], (TOKENS, HEADS), jnp.float32) ** block_levels(part_splits[8], (TOKENS, HEADS), ((0, 8), (1, 2)), -0.2, 0.2)), 0.1, 1.0),
        "w_in": gaussian(seeds[9], (HEADS, 2 * FH, DH), DH ** -0.5, 0.25, ((0, 2), (2, 8)), jnp.float32),
        "w_out": gaussian(seeds[10], (HEADS, FH, DH), FH ** -0.5, 0.3125, ((0, 2), (2, 8)), jnp.float32),
        "momentum_in": draw_momentum_in(jax.random.fold_in(jax.random.fold_in(seeds[14], part), 71), part),
        "momentum_out": draw_momentum_out(jax.random.fold_in(jax.random.fold_in(seeds[14], part), 71), part),
        "step_size": jnp.clip(jnp.exp(math.log(0.06) - 1.0986123 * jax.random.uniform(seeds[13], (HEADS,), jnp.float32) ** block_levels(seeds[13], (HEADS,), ((0, 2),), -0.2, 0.2)), 0.02, 0.06),
    }


def silu_grad(inputs):
    sigmoid_val = jax.nn.sigmoid(inputs)
    return sigmoid_val * (1.0 + inputs * (1.0 - sigmoid_val))

def attention(attn_query, attn_key, attn_value, lookback, frame_start):
    reach_rows = (WINDOW + TOK_DEV - 2) // TOK_DEV * TOK_DEV
    block_count = TOKENS // TOK_DEV
    col_count = ATT_HEADS * ATT_DIM
    key_padded = jnp.concatenate([jnp.zeros((reach_rows, col_count), attn_key.dtype), attn_key], axis=0)
    value_padded = jnp.concatenate([jnp.zeros((reach_rows, col_count), attn_value.dtype), attn_value], axis=0)
    scale_factor = 1.0 / math.sqrt(ATT_DIM)

    def one_block(block_idx):
        first_row = (block_idx * TOK_DEV).astype(jnp.int32)
        query_blk = lax.dynamic_slice_in_dim(attn_query, first_row, TOK_DEV, 0).reshape(TOK_DEV, ATT_HEADS, ATT_DIM)
        key_blk = lax.dynamic_slice_in_dim(key_padded, first_row, reach_rows + TOK_DEV, 0).reshape(-1, ATT_HEADS, ATT_DIM)
        value_blk = lax.dynamic_slice_in_dim(value_padded, first_row, reach_rows + TOK_DEV, 0).reshape(-1, ATT_HEADS, ATT_DIM)
        look_back = lax.dynamic_slice_in_dim(lookback, first_row, TOK_DEV, 0)
        frame_first = lax.dynamic_slice_in_dim(frame_start, first_row, TOK_DEV, 0)
        query_pos = first_row + jnp.arange(TOK_DEV, dtype=jnp.int32)
        key_pos = first_row - reach_rows + jnp.arange(reach_rows + TOK_DEV, dtype=jnp.int32)
        low_bound = jnp.maximum(frame_first, query_pos - look_back + 1)
        allowed = (key_pos[None, :] >= low_bound[:, None]) & (key_pos[None, :] <= query_pos[:, None])
        scores = jnp.einsum('qhd,khd->hqk', query_blk.astype(jnp.float32), key_blk.astype(jnp.float32)) * scale_factor
        scores = jnp.where(allowed[None], scores, jnp.float32(-1e+30))
        row_peak = lax.optimization_barrier(jnp.max(scores, axis=2, keepdims=True))
        exp_scores = jnp.exp(scores - row_peak)
        row_total = lax.optimization_barrier(jnp.sum(exp_scores, axis=2, keepdims=True))
        attn_weights = (exp_scores / row_total).astype(jnp.bfloat16)
        result = jnp.einsum('hqk,khd->qhd', attn_weights.astype(jnp.float32), value_blk.astype(jnp.float32))
        return result.reshape(TOK_DEV, col_count).astype(jnp.bfloat16)
    outputs = lax.map(one_block, jnp.arange(block_count, dtype=jnp.int32))
    return outputs.reshape(TOKENS, col_count)

def fast_hidden(tokens, weights_in):
    mixed = jnp.dot(tokens, weights_in.T, preferred_element_type=jnp.float32)
    return (mixed[:, :FH], mixed[:, FH:])

def reference(attn_query, attn_key, attn_value, lookback, frame_start, fast_query, fast_key, fast_value, token_rate, w_in, w_out, momentum_in, momentum_out, step_size):
    attn_out = attention(attn_query, attn_key, attn_value, lookback, frame_start)
    w_in_b = w_in.astype(jnp.bfloat16)
    w_out_b = w_out.astype(jnp.bfloat16)
    block_count = TOKENS // TOK_DEV
    rate_norm = 1.0 / math.sqrt(TOKENS)
    grads_in = []
    grads_out = []
    for head_idx in range(HEADS):
        key_head = fast_key[:, head_idx * DH:(head_idx + 1) * DH].reshape(block_count, TOK_DEV, DH)
        value_head = fast_value[:, head_idx * DH:(head_idx + 1) * DH].reshape(block_count, TOK_DEV, DH)
        rate_head = token_rate[:, head_idx].reshape(block_count, TOK_DEV)
        weights_in = w_in_b[head_idx]
        weights_out = w_out_b[head_idx]

        def scan_step(totals, block_data):
            key_rows, value_rows, rate_rows = block_data
            gate_part, up_part = fast_hidden(key_rows, weights_in)
            hidden = (jax.nn.silu(gate_part) * up_part).astype(jnp.bfloat16)
            out_grad = (-(rate_rows[:, None] * rate_norm) * value_rows.astype(jnp.float32)).astype(jnp.bfloat16)
            grad_out = totals[1] + jnp.dot(hidden.T, out_grad, preferred_element_type=jnp.float32)
            hid_grad = jnp.dot(out_grad, weights_out.T, preferred_element_type=jnp.float32)
            gate_grad = hid_grad * up_part * silu_grad(gate_part)
            up_grad = hid_grad * jax.nn.silu(gate_part)
            mix_grad = jnp.concatenate([gate_grad, up_grad], axis=1).astype(jnp.bfloat16)
            grad_in = totals[0] + jnp.dot(mix_grad.T, key_rows, preferred_element_type=jnp.float32)
            return ((grad_in, grad_out), None)
        start_totals = (jnp.zeros((2 * FH, DH), jnp.float32), jnp.zeros((FH, DH), jnp.float32))
        (grad_in, grad_out), _ = lax.scan(scan_step, start_totals, (key_head, value_head, rate_head))
        grads_in.append(grad_in)
        grads_out.append(grad_out)
    new_momentum_in = 0.9 * momentum_in + jnp.stack(grads_in)
    new_momentum_out = 0.9 * momentum_out + jnp.stack(grads_out)
    norm_in = lax.rsqrt(lax.optimization_barrier(jnp.mean(new_momentum_in * new_momentum_in, axis=2, keepdims=True)) + 1e-06)
    norm_out = lax.rsqrt(lax.optimization_barrier(jnp.mean(new_momentum_out * new_momentum_out, axis=2, keepdims=True)) + 1e-06)
    new_w_in = w_in - step_size[:, None, None] * (new_momentum_in * norm_in)
    new_w_out = w_out - step_size[:, None, None] * (new_momentum_out * norm_out)
    new_in_b = new_w_in.astype(jnp.bfloat16)
    new_out_b = new_w_out.astype(jnp.bfloat16)
    head_outs = []
    for head_idx in range(HEADS):
        query_head = fast_query[:, head_idx * DH:(head_idx + 1) * DH].reshape(block_count, TOK_DEV, DH)
        weights_in = new_in_b[head_idx]
        weights_out = new_out_b[head_idx]

        def apply_block(query_rows):
            gate_part, up_part = fast_hidden(query_rows, weights_in)
            query_hidden = (jax.nn.silu(gate_part) * up_part).astype(jnp.bfloat16)
            return jnp.dot(query_hidden, weights_out, preferred_element_type=jnp.float32).astype(jnp.bfloat16)
        head_outs.append(lax.map(apply_block, query_head).reshape(TOKENS, DH))
    fast_out = jnp.concatenate(head_outs, axis=1)
    return (attn_out, fast_out, new_w_in, new_w_out, new_momentum_in, new_momentum_out)
```

```python
import functools
import math

import jax
import jax.numpy as jnp
from jax import lax
from jax.experimental import pallas as pl
from jax.experimental.pallas import tpu as pltpu
from jax.sharding import PartitionSpec as P

ATT_DIM = 128
DH = 512
FH = 320
WINDOW = 768
AXIS = "ctx"
VMEM = pltpu.MemorySpace.VMEM
SMEM = pltpu.MemorySpace.SMEM
F32 = jnp.float32
BF16 = jnp.bfloat16


def moved(value, steps):
    count = lax.axis_size(AXIS)
    return lax.ppermute(value, AXIS, [(i, i + steps) for i in range(count - steps)])


def swapped(value, bits):
    return lax.ppermute(value, AXIS, [(i, i ^ bits) for i in range(lax.axis_size(AXIS))])


def call(kernel, out_shape, operands, smem=(), scratch=(), limit=24 << 20, cost=None):
    in_specs = [
        pl.BlockSpec(memory_space=SMEM if i in smem else VMEM) for i in range(len(operands))
    ]
    out_specs = jax.tree.map(lambda _: pl.BlockSpec(memory_space=VMEM), out_shape)
    return pl.pallas_call(
        kernel,
        out_shape=out_shape,
        in_specs=in_specs,
        out_specs=out_specs,
        scratch_shapes=list(scratch),
        compiler_params=pltpu.CompilerParams(vmem_limit_bytes=limit),
        cost_estimate=cost,
    )(*operands)


def window_blocks(attn_key, attn_value):
    rows = attn_key.shape[0]
    steps_back = (WINDOW + rows - 2) // rows
    own = jnp.concatenate([attn_key, attn_value], axis=0)
    even = lax.axis_index(AXIS) % 2 == 0
    blocks = {0: own}
    for distance in range(2, steps_back + 2, 2):
        if distance <= steps_back + 1:
            blocks[distance] = moved(blocks[distance - 2], 2)
    out = {d: blocks[d] for d in range(2, steps_back + 1, 2)}
    for distance in range(1, steps_back + 1, 2):
        out[distance] = swapped(jnp.where(even, blocks[distance - 1], blocks[distance + 1]), 1)
    return [out[d] for d in range(steps_back, 0, -1)]


def attention_kernel(count, low_ref, q_ref, k_ref, v_ref, *refs):
    blocks, o_ref, bias_ref = refs[:count], refs[count], refs[count + 1]
    rows = q_ref.shape[0]
    keys = bias_ref.shape[1]

    @pl.when(pl.program_id(0) == 0)
    def _():
        key_pos = lax.broadcasted_iota(jnp.int32, (rows, keys), 1) - count * rows
        query_pos = lax.broadcasted_iota(jnp.int32, (rows, keys), 0)
        seen = (key_pos >= low_ref[...]) & (key_pos <= query_pos)
        bias_ref[...] = jnp.where(seen, 0.0, -1e30).astype(F32)

    for head in range(q_ref.shape[1] // ATT_DIM):
        cols = slice(head * ATT_DIM, (head + 1) * ATT_DIM)
        key_all = jnp.concatenate([b[:rows, cols] for b in blocks] + [k_ref[:, cols]], axis=0)
        value_all = jnp.concatenate([b[rows:, cols] for b in blocks] + [v_ref[:, cols]], axis=0)
        scores = lax.dot_general(
            q_ref[:, cols], key_all, (((1,), (1,)), ((), ())), preferred_element_type=F32
        )
        scores = scores * (1.0 / math.sqrt(ATT_DIM)) + bias_ref[...]
        weights = jnp.exp(scores - jnp.max(scores, axis=1, keepdims=True))
        total = jnp.sum(weights, axis=1, keepdims=True)
        result = jnp.dot(weights.astype(BF16), value_all, preferred_element_type=F32)
        o_ref[:, cols] = (result / total).astype(BF16)


def attend(attn_query, attn_key, attn_value, lookback, frame_start):
    rows, width = attn_query.shape
    anchor = lax.axis_index(AXIS) * rows
    query_pos = jnp.arange(rows, dtype=jnp.int32)
    low = jnp.maximum(frame_start - anchor, query_pos - lookback + 1)[:, None]
    blocks = window_blocks(attn_key, attn_value)
    count = len(blocks)
    step = 2 * ATT_DIM if width % (2 * ATT_DIM) == 0 else ATT_DIM
    keys = (count + 1) * rows
    head_cols = pl.BlockSpec((rows, step), lambda i: (0, i))
    return pl.pallas_call(
        functools.partial(attention_kernel, count),
        grid=(width // step,),
        out_shape=jax.ShapeDtypeStruct((rows, width), BF16),
        in_specs=[pl.BlockSpec((rows, 1), lambda i: (0, 0))]
        + [head_cols] * 3
        + [pl.BlockSpec((2 * rows, step), lambda i: (0, i))] * count,
        out_specs=head_cols,
        scratch_shapes=[pltpu.VMEM((rows, keys), F32)],
        compiler_params=pltpu.CompilerParams(vmem_limit_bytes=24 << 20),
        cost_estimate=pl.CostEstimate(
            flops=4 * rows * keys * width,
            bytes_accessed=4 * (keys + rows) * width,
            transcendentals=rows * keys * width // ATT_DIM,
        ),
    )(low, attn_query, attn_key, attn_value, *blocks)


def in_cols(head):
    return slice(head * 2 * FH, (head + 1) * 2 * FH)


def out_cols(heads, head):
    return slice((2 * heads + head) * FH, (2 * heads + head + 1) * FH)


def pack_kernel(in_ref, out_ref, packed_ref):
    heads = in_ref.shape[0]
    for head in range(heads):
        packed_ref[:, in_cols(head)] = in_ref[head].astype(BF16)
        packed_ref[:, out_cols(heads, head)] = out_ref[head].astype(BF16)


def place(index_ref, offsets, parts, whole_ref):
    for bits, part in zip(offsets, parts, strict=True):
        rows = part.shape[0]
        start = pl.multiple_of((index_ref[0] ^ bits) * rows, rows)
        whole_ref[pl.ds(start, rows), :] = part[...]


def gradient_kernel(offsets, rate_norm, index_ref, key_ref, value_ref, rate_ref, *refs):
    count = len(offsets)
    parts, grads = refs[:count], refs[count : 2 * count]
    w_ref, g_ref = refs[2 * count :]
    heads = rate_ref.shape[1]
    place(index_ref, offsets, parts, w_ref)
    for head in range(heads):
        cols = slice(head * DH, (head + 1) * DH)
        keys = key_ref[:, cols]
        mixed = jnp.dot(keys, w_ref[:, in_cols(head)], preferred_element_type=F32)
        gate, up = mixed[:, :FH], mixed[:, FH:]
        sig = jax.nn.sigmoid(gate)
        silu = gate * sig
        hidden = (silu * up).astype(BF16)
        rate = -(rate_ref[:, head : head + 1] * rate_norm)
        out_grad = (rate * value_ref[:, cols].astype(F32)).astype(BF16)
        grad_out = lax.dot_general(
            out_grad, hidden, (((0,), (0,)), ((), ())), preferred_element_type=F32
        )
        g_ref[:, out_cols(heads, head)] = grad_out.astype(BF16)
        hid_grad = jnp.dot(out_grad, w_ref[:, out_cols(heads, head)], preferred_element_type=F32)
        gate_grad = hid_grad * up * (sig * (1.0 + gate * (1.0 - sig)))
        mix_grad = jnp.concatenate([gate_grad, hid_grad * silu], axis=1).astype(BF16)
        grad_in = lax.dot_general(
            keys, mix_grad, (((0,), (0,)), ((), ())), preferred_element_type=F32
        )
        g_ref[:, in_cols(head)] = grad_in.astype(BF16)
    for bits, grad in zip(offsets, grads, strict=True):
        rows = grad.shape[0]
        start = pl.multiple_of((index_ref[0] ^ bits) * rows, rows)
        grad[...] = g_ref[pl.ds(start, rows), :]


def momentum_kernel(count, *refs):
    parts = refs[:count]
    old_in, old_out, new_in, new_out, packed = refs[count:]
    heads = old_in.shape[0]
    for head in range(heads):
        for old, new, cols in (
            (old_in, new_in, in_cols(head)),
            (old_out, new_out, out_cols(heads, head)),
        ):
            grad = parts[0][:, cols].astype(F32)
            for part in parts[1:]:
                grad = grad + part[:, cols].astype(F32)
            fresh = 0.9 * old[head] + grad
            new[head] = fresh
            packed[:, cols] = fresh.astype(BF16)


def apply_kernel(offsets, index_ref, step_ref, query_ref, *refs):
    count = len(offsets)
    weights, momenta = refs[:count], refs[count : 2 * count]
    w_in, w_out, m_in, m_out, fast_ref, new_in, new_out, w_ref = refs[2 * count :]
    heads = w_in.shape[0]
    square = None
    for part in momenta:
        value = part[...].astype(F32)
        term = jnp.sum(value * value, axis=0, keepdims=True)
        square = term if square is None else square + term
    norm = lax.rsqrt(square * (1.0 / DH) + 1e-06)
    lane = lax.broadcasted_iota(jnp.int32, norm.shape, 1)
    scale = jnp.zeros_like(norm)
    for head in range(heads):
        for cols in (in_cols(head), out_cols(heads, head)):
            scale = jnp.where((lane >= cols.start) & (lane < cols.stop), step_ref[head], scale)
    scale = scale * norm
    for bits, weight, momentum in zip(offsets, weights, momenta, strict=True):
        rows = weight.shape[0]
        start = pl.multiple_of((index_ref[0] ^ bits) * rows, rows)
        fresh = weight[...].astype(F32) - momentum[...].astype(F32) * scale
        w_ref[pl.ds(start, rows), :] = fresh.astype(BF16)
    for head in range(heads):
        cols = slice(head * DH, (head + 1) * DH)
        new_in[head] = w_in[head] - m_in[head] * scale[:, in_cols(head)]
        new_out[head] = w_out[head] - m_out[head] * scale[:, out_cols(heads, head)]
        mixed = jnp.dot(query_ref[:, cols], w_ref[:, in_cols(head)], preferred_element_type=F32)
        gate, up = mixed[:, :FH], mixed[:, FH:]
        hidden = (gate * jax.nn.sigmoid(gate) * up).astype(BF16)
        result = lax.dot_general(
            hidden,
            w_ref[:, out_cols(heads, head)],
            (((1,), (1,)), ((), ())),
            preferred_element_type=F32,
        )
        fast_ref[:, cols] = result.astype(BF16)


def gathered(part):
    count = lax.axis_size(AXIS)
    parts = {0: part}
    for bits in range(2, count, 2):
        parts[bits] = swapped(part, bits)
    for bits in range(0, count, 2):
        parts[bits + 1] = swapped(parts[bits], 1)
    return [parts[bits] for bits in range(count)]


def scattered(parts):
    count = len(parts)
    terms = []
    for bits in range(count - 2, -1, -2):
        pair = parts[bits].astype(F32) + swapped(parts[bits + 1], 1).astype(F32)
        pair = pair.astype(BF16)
        terms.append(swapped(pair, bits) if bits else pair)
    return terms


def fast_layer(fast_query, fast_key, fast_value, token_rate, w_in, w_out, m_in, m_out, step_size):
    count = lax.axis_size(AXIS)
    rows = fast_key.shape[0]
    heads, _, share = w_in.shape
    columns = 3 * heads * FH
    by_pairs = count & (count - 1) == 0 and count > 1 and share % 16 == 0
    shape = jax.ShapeDtypeStruct
    w_in, w_out, m_in, m_out = (jnp.swapaxes(a, 1, 2) for a in (w_in, w_out, m_in, m_out))
    index = lax.axis_index(AXIS).astype(jnp.int32)[None]
    packed = call(pack_kernel, shape((share, columns), BF16), (w_in, w_out))
    if by_pairs:
        offsets, weights = tuple(range(count)), gathered(packed)
    else:
        offsets, weights, index = (0,), [lax.all_gather(packed, AXIS, axis=0, tiled=True)], index * 0
    part_shape = shape(weights[0].shape, BF16)
    full = pltpu.VMEM((DH, columns), BF16)
    grads = call(
        functools.partial(gradient_kernel, offsets, 1.0 / math.sqrt(rows * count)),
        [part_shape] * len(offsets),
        (index, fast_key, fast_value, token_rate, *weights),
        smem=(0,),
        scratch=(full, full),
        cost=pl.CostEstimate(
            flops=12 * rows * DH * FH * heads,
            bytes_accessed=4 * DH * columns + 4 * rows * DH * heads,
            transcendentals=rows * FH * heads,
        ),
    )
    if by_pairs:
        terms = scattered(grads)
    else:
        terms = [lax.psum_scatter(grads[0].astype(F32), AXIS, scatter_dimension=0, tiled=True)]
    new_m_in, new_m_out, packed_m = call(
        functools.partial(momentum_kernel, len(terms)),
        [shape(m_in.shape, F32), shape(m_out.shape, F32), shape((share, columns), BF16)],
        (*terms, m_in, m_out),
    )
    if by_pairs:
        momenta = gathered(packed_m)
    else:
        momenta = [lax.all_gather(packed_m, AXIS, axis=0, tiled=True)]
    fast_out, new_w_in, new_w_out = call(
        functools.partial(apply_kernel, offsets),
        [shape(fast_query.shape, BF16), shape(w_in.shape, F32), shape(w_out.shape, F32)],
        (index, step_size, fast_query, *weights, *momenta, w_in, w_out, new_m_in, new_m_out),
        smem=(0, 1),
        scratch=(full,),
        cost=pl.CostEstimate(
            flops=6 * rows * DH * FH * heads,
            bytes_accessed=4 * DH * columns + 4 * rows * DH * heads,
            transcendentals=rows * FH * heads,
        ),
    )
    outs = (new_w_in, new_w_out, new_m_in, new_m_out)
    return (fast_out, *(jnp.swapaxes(a, 1, 2) for a in outs))


def body(
    attn_query,
    attn_key,
    attn_value,
    lookback,
    frame_start,
    fast_query,
    fast_key,
    fast_value,
    token_rate,
    w_in,
    w_out,
    momentum_in,
    momentum_out,
    step_size,
):
    fast = fast_layer(
        fast_query,
        fast_key,
        fast_value,
        token_rate,
        w_in,
        w_out,
        momentum_in,
        momentum_out,
        step_size,
    )
    attn_out = attend(attn_query, attn_key, attn_value, lookback, frame_start)
    return (attn_out, *fast)


def solution(mesh):
    tokens, weights = P(("groups", "ctx"), "head"), P("head", None, "ctx")
    state = P(("groups", "head"), None, "ctx")
    positions = P(("groups", "ctx"))
    return jax.shard_map(
        body,
        mesh=mesh,
        in_specs=(
            (tokens,) * 3 + (positions,) * 2 + (tokens,) * 4 + (weights,) * 2 + (state,) * 2
        )
        + (P("head"),),
        out_specs=(tokens,) * 2 + (state,) * 4,
        check_vma=False,
    )
```

```python
import functools
import math

import jax
import jax.numpy as jnp
from jax import lax
from jax.experimental import pallas as pl
from jax.experimental.pallas import tpu as pltpu
from jax.sharding import PartitionSpec as P


ATT_DIM = 128
DH = 512
FH = 320
WINDOW = 768
AXIS = "ctx"
GROUPS = "groups"
F32 = jnp.float32
BF16 = jnp.bfloat16
ANY = pl.BlockSpec(memory_space=pl.ANY)
SCALARS = pl.BlockSpec(memory_space=pltpu.MemorySpace.SMEM)


def moved(value, steps):
    count = lax.axis_size(AXIS)
    return lax.ppermute(value, AXIS, [(i, i + steps) for i in range(count - steps)])


def swapped(value, bits):
    return lax.ppermute(value, AXIS, [(i, i ^ bits) for i in range(lax.axis_size(AXIS))])


def sent(value, even):
    count = lax.axis_size(AXIS)
    return lax.ppermute(value, AXIS, [(i, i ^ 1) for i in range(0 if even else 1, count, 2)])


def across(value, bits_of):
    groups, count = lax.axis_size(GROUPS), lax.axis_size(AXIS)
    pairs = []
    for group in range(groups):
        bits, flip = bits_of(group)
        for place in range(count):
            pairs.append((group * count + place, (group ^ flip) * count + (place ^ bits)))
    return lax.ppermute(value, (GROUPS, AXIS), pairs)


def call(kernel, out_shape, operands, smem=(), scratch=(), copies=0, limit=16 << 20, cost=None):
    return pl.pallas_call(
        kernel,
        out_shape=out_shape,
        in_specs=[SCALARS if i in smem else ANY for i in range(len(operands))],
        out_specs=jax.tree.map(lambda _: ANY, out_shape),
        scratch_shapes=[*scratch, pltpu.SemaphoreType.DMA((copies,))],
        compiler_params=pltpu.CompilerParams(vmem_limit_bytes=limit),
        cost_estimate=cost,
    )(*operands)


class Copies:
    def __init__(self, sems):
        self.sems, self.used = sems, 0

    def make(self, source, target):
        copy = pltpu.make_async_copy(source, target, self.sems.at[self.used])
        self.used += 1
        return copy

    def start(self, source, target):
        copy = self.make(source, target)
        copy.start()
        return copy


def wait_all(copies):
    for copy in copies:
        copy.wait()


def window_blocks(rows, value):
    steps_back = (WINDOW + rows - 2) // rows
    reach = (steps_back + 1) // 2
    evens = [value]
    for _ in range(1, reach + 1):
        evens.append(moved(evens[-1], 2))
    odds = [sent(evens[0], True)]
    odds += [swapped(evens[j], 1) for j in range(1, reach)]
    odds.append(sent(evens[reach], False))
    return evens[1 : steps_back // 2 + 1], odds


def attention_kernel(steps_back, chunks, index_ref, *refs):
    half, reach = steps_back // 2, (steps_back + 1) // 2
    low_ref, q_ref, k_ref, v_ref = refs[:4]
    per = half + reach + 1
    streams = (refs[4 : 4 + per], refs[4 + per : 4 + 2 * per])
    o_ref, low, q, k, v, o, bias, sems = refs[4 + 2 * per :]
    rows, width = q.shape
    keys = k.shape[0]
    even = index_ref[0] % 2 == 0
    copies = Copies(sems)
    first = copies.start(low_ref, low)
    waits = []
    step = width // chunks
    for chunk in range(chunks):
        cols = pl.ds(chunk * step, step)
        todo = [copies.start(q_ref.at[:, cols], q.at[:, cols])]
        for own, stream, whole in ((k_ref, streams[0], k), (v_ref, streams[1], v)):
            todo.append(
                copies.start(own.at[:, cols], whole.at[pl.ds(steps_back * rows, rows), cols])
            )
            for j in range(1, half + 1):
                slot = pl.ds((steps_back - 2 * j) * rows, rows)
                todo.append(copies.start(stream[j - 1].at[:, cols], whole.at[slot, cols]))
            for j in range(reach + 1):
                source = stream[half + j].at[:, cols]
                back = 2 * j + jnp.where(even, -1, 1)
                if j == 0 or j == reach:
                    slot = pl.ds((steps_back - (1 if j == 0 else 2 * j - 1)) * rows, rows)
                    copy = copies.make(source, whole.at[slot, cols])
                    here = even if j else jnp.logical_not(even)
                    pl.when(here)(copy.start)
                    todo.append((here, copy))
                else:
                    start = pl.multiple_of((steps_back - back) * rows, rows)
                    todo.append(copies.start(source, whole.at[pl.ds(start, rows), cols]))
        waits.append(todo)
    first.wait()
    key_pos = lax.broadcasted_iota(jnp.int32, (rows, keys), 1) - steps_back * rows
    query_pos = lax.broadcasted_iota(jnp.int32, (rows, keys), 0)
    seen = (key_pos >= low[...]) & (key_pos <= query_pos)
    bias[...] = jnp.where(seen, 0.0, -1e30).astype(F32)
    outs = []
    for chunk in range(chunks):
        for copy in waits[chunk]:
            if isinstance(copy, tuple):
                pl.when(copy[0])(copy[1].wait)
            else:
                copy.wait()
        for head in range(chunk * step // ATT_DIM, (chunk + 1) * step // ATT_DIM):
            cols = slice(head * ATT_DIM, (head + 1) * ATT_DIM)
            scores = lax.dot_general(
                q[:, cols], k[:, cols], (((1,), (1,)), ((), ())), preferred_element_type=F32
            )
            scores = scores * (1.0 / math.sqrt(ATT_DIM)) + bias[...]
            weights = jnp.exp(scores - jnp.max(scores, axis=1, keepdims=True))
            total = jnp.sum(weights, axis=1, keepdims=True)
            result = jnp.dot(weights.astype(BF16), v[:, cols], preferred_element_type=F32)
            o[:, cols] = (result / total).astype(BF16)
        cols = pl.ds(chunk * step, step)
        outs.append(copies.start(o.at[:, cols], o_ref.at[:, cols]))
    wait_all(outs)


def attend(index, attn_query, attn_key, attn_value, lookback, frame_start):
    rows, width = attn_query.shape
    steps_back = (WINDOW + rows - 2) // rows
    query_pos = jnp.arange(rows, dtype=jnp.int32)
    low = jnp.maximum(frame_start - index[0] * rows, query_pos - lookback + 1)[:, None]
    evens, odds = window_blocks(rows, attn_key)
    evens_v, odds_v = window_blocks(rows, attn_value)
    blocks = (*evens, *odds, *evens_v, *odds_v)
    keys = (steps_back + 1) * rows
    chunks = 2 if width % (2 * ATT_DIM) == 0 else 1
    return call(
        functools.partial(attention_kernel, steps_back, chunks),
        jax.ShapeDtypeStruct((rows, width), BF16),
        (index, low, attn_query, attn_key, attn_value, *blocks),
        smem=(0,),
        scratch=(
            pltpu.VMEM((rows, 1), jnp.int32),
            pltpu.VMEM((rows, width), BF16),
            pltpu.VMEM((keys, width), BF16),
            pltpu.VMEM((keys, width), BF16),
            pltpu.VMEM((rows, width), BF16),
            pltpu.VMEM((rows, keys), F32),
        ),
        copies=1 + chunks * (4 + len(blocks)),
        cost=pl.CostEstimate(
            flops=4 * rows * keys * width,
            bytes_accessed=4 * (keys + rows) * width,
            transcendentals=rows * keys * width // ATT_DIM,
        ),
    )


def in_cols(head):
    return slice(head * 2 * FH, (head + 1) * 2 * FH)


def out_cols(heads, head):
    return slice((2 * heads + head) * FH, (2 * heads + head + 1) * FH)


def pack_kernel(in_hbm, out_hbm, packed_hbm, w_in, w_out, packed, sems):
    copies = Copies(sems)
    wait_all([copies.start(in_hbm, w_in), copies.start(out_hbm, w_out)])
    heads = w_in.shape[0]
    for head in range(heads):
        packed[:, in_cols(head)] = w_in[head].astype(BF16)
        packed[:, out_cols(heads, head)] = w_out[head].astype(BF16)
    copies.start(packed, packed_hbm).wait()


def share_of(starts_ref, place, rows):
    return pl.ds(pl.multiple_of(starts_ref[place], rows), rows)


def gradient_kernel(count, rate_norm, starts_ref, key_hbm, value_hbm, rate_hbm, *refs):
    parts, grads = refs[:count], refs[count : 2 * count]
    key_ref, value_ref, rate_ref, w_ref, g_ref, sems = refs[2 * count :]
    rows = parts[0].shape[0]
    heads = rate_ref.shape[1]
    copies = Copies(sems)
    todo = [
        copies.start(source, target)
        for source, target in ((key_hbm, key_ref), (value_hbm, value_ref), (rate_hbm, rate_ref))
    ]
    for place, part in enumerate(parts):
        todo.append(copies.start(part, w_ref.at[share_of(starts_ref, place, rows)]))
    wait_all(todo)
    for head in range(heads):
        cols = slice(head * DH, (head + 1) * DH)
        keys = key_ref[:, cols]
        mixed = jnp.dot(keys, w_ref[:, in_cols(head)], preferred_element_type=F32)
        gate, up = mixed[:, :FH], mixed[:, FH:]
        sig = jax.nn.sigmoid(gate)
        silu = gate * sig
        hidden = (silu * up).astype(BF16)
        rate = -(rate_ref[:, head : head + 1] * rate_norm)
        out_grad = (rate * value_ref[:, cols].astype(F32)).astype(BF16)
        grad_out = lax.dot_general(
            out_grad, hidden, (((0,), (0,)), ((), ())), preferred_element_type=F32
        )
        g_ref[:, out_cols(heads, head)] = grad_out.astype(BF16)
        hid_grad = jnp.dot(out_grad, w_ref[:, out_cols(heads, head)], preferred_element_type=F32)
        gate_grad = hid_grad * up * (sig * (1.0 + gate * (1.0 - sig)))
        mix_grad = jnp.concatenate([gate_grad, hid_grad * silu], axis=1).astype(BF16)
        grad_in = lax.dot_general(
            keys, mix_grad, (((0,), (0,)), ((), ())), preferred_element_type=F32
        )
        g_ref[:, in_cols(head)] = grad_in.astype(BF16)
    wait_all(
        [
            copies.start(g_ref.at[share_of(starts_ref, count + place, rows)], grad)
            for place, grad in enumerate(grads)
        ]
    )


def momentum_kernel(count, *refs):
    ins, outs, held = refs[: count + 2], refs[count + 2 : count + 5], refs[count + 5 : -1]
    copies = Copies(refs[-1])
    wait_all([copies.start(s, t) for s, t in zip(ins, held[: count + 2], strict=True)])
    parts = held[:count]
    old_in, old_out, new_in, new_out, packed = held[count:]
    heads = old_in.shape[0]
    for head in range(heads):
        for old, new, cols in (
            (old_in, new_in, in_cols(head)),
            (old_out, new_out, out_cols(heads, head)),
        ):
            grad = parts[0][:, cols].astype(F32)
            for part in parts[1:]:
                grad = grad + part[:, cols].astype(F32)
            fresh = 0.9 * old[head] + grad
            new[head] = fresh
            packed[:, cols] = fresh.astype(BF16)
    wait_all(
        [copies.start(s, t) for s, t in zip((new_in, new_out, packed), outs, strict=True)]
    )


def apply_kernel(count, starts_ref, step_ref, query_hbm, *refs):
    weights, momenta, state = refs[:count], refs[count : 2 * count], refs[2 * count : 2 * count + 4]
    fast_hbm, new_in_hbm, new_out_hbm = refs[2 * count + 4 : 2 * count + 7]
    query_ref, w_in, w_out, m_in, m_out, w_ref, m_ref, fast_ref, sems = refs[2 * count + 7 :]
    rows = weights[0].shape[0]
    heads = w_in.shape[0]
    copies = Copies(sems)
    got_m, got_w = [], []
    for place, part in enumerate(momenta):
        got_m.append(copies.start(part, m_ref.at[share_of(starts_ref, 2 * count + place, rows)]))
    for place, part in enumerate(weights):
        got_w.append(copies.start(part, w_ref.at[share_of(starts_ref, place, rows)]))
    for source, target in zip((query_hbm, *state), (query_ref, w_in, w_out, m_in, m_out), strict=True):
        got_w.append(copies.start(source, target))
    wait_all(got_m)
    block = DH // 8
    square = None
    for place in range(8):
        value = m_ref[place * block : (place + 1) * block].astype(F32)
        term = jnp.sum(value * value, axis=0, keepdims=True)
        square = term if square is None else square + term
    norm = lax.rsqrt(square * (1.0 / DH) + 1e-06)
    lane = lax.broadcasted_iota(jnp.int32, norm.shape, 1)
    scale = jnp.zeros_like(norm)
    for head in range(heads):
        for cols in (in_cols(head), out_cols(heads, head)):
            scale = jnp.where((lane >= cols.start) & (lane < cols.stop), step_ref[head], scale)
    scale = scale * norm
    wait_all(got_w)
    for place in range(8):
        part = slice(place * block, (place + 1) * block)
        fresh = w_ref[part].astype(F32) - m_ref[part].astype(F32) * scale
        w_ref[part] = fresh.astype(BF16)
    outs = []
    for head in range(heads):
        w_in[head] = w_in[head] - m_in[head] * scale[:, in_cols(head)]
        w_out[head] = w_out[head] - m_out[head] * scale[:, out_cols(heads, head)]
    outs.append(copies.start(w_in, new_in_hbm))
    outs.append(copies.start(w_out, new_out_hbm))
    for head in range(heads):
        cols = slice(head * DH, (head + 1) * DH)
        mixed = jnp.dot(query_ref[:, cols], w_ref[:, in_cols(head)], preferred_element_type=F32)
        gate, up = mixed[:, :FH], mixed[:, FH:]
        hidden = (gate * jax.nn.sigmoid(gate) * up).astype(BF16)
        result = lax.dot_general(
            hidden,
            w_ref[:, out_cols(heads, head)],
            (((1,), (1,)), ((), ())),
            preferred_element_type=F32,
        )
        fast_ref[:, cols] = result.astype(BF16)
    outs.append(copies.start(fast_ref, fast_hbm))
    wait_all(outs)


def gathered(part):
    count = lax.axis_size(AXIS)
    parts = {0: part}
    for bits in range(2, count, 2):
        parts[bits] = swapped(part, bits)
    for bits in range(0, count, 2):
        parts[bits + 1] = swapped(parts[bits], 1)
    return list(parts.values()), list(parts)


def gathered_twin(part):
    group = lax.axis_index(GROUPS) % 2
    near = swapped(part, 2)
    far = across(part, lambda g: (4 + 2 * (g % 2), 0))
    own_x = swapped(part, 1)
    near_x = swapped(near, 1)
    far_y = across(far, lambda g: (0, 1))
    far_x = swapped(far, 1)
    far_xy = across(far_x, lambda g: (0, 1))
    mine, other = 4 + 2 * group, 6 - 2 * group
    return [part, near, own_x, near_x, far, far_y, far_x, far_xy], [
        0, 2, 1, 3, mine, other, mine + 1, other + 1,
    ]


def scattered(parts):
    count = len(parts)
    terms = []
    for bits in range(count - 2, -1, -2):
        pair = parts[bits].astype(F32) + swapped(parts[bits + 1], 1).astype(F32)
        pair = pair.astype(BF16)
        terms.append(swapped(pair, bits) if bits else pair)
    return terms


def fast_layer(
    index, fast_query, fast_key, fast_value, token_rate, w_in, w_out, m_in, m_out, step_size, before_apply
):
    count = lax.axis_size(AXIS)
    rows = fast_key.shape[0]
    heads, _, share = w_in.shape
    columns = 3 * heads * FH
    by_pairs = count & (count - 1) == 0 and count > 1 and share % 16 == 0
    shape = jax.ShapeDtypeStruct
    w_in, w_out, m_in, m_out = (jnp.swapaxes(a, 1, 2) for a in (w_in, w_out, m_in, m_out))
    part = (share, columns)
    packed = call(
        pack_kernel,
        shape(part, BF16),
        (w_in, w_out),
        scratch=(
            pltpu.VMEM(w_in.shape, F32),
            pltpu.VMEM(w_out.shape, F32),
            pltpu.VMEM(part, BF16),
        ),
        copies=3,
    )
    if not by_pairs:
        weights, bits = [lax.all_gather(packed, AXIS, axis=0, tiled=True)], None
    elif count == 8 and lax.axis_size(GROUPS) % 2 == 0:
        weights, bits = gathered_twin(packed)
    else:
        weights, bits = gathered(packed)
    pieces = len(weights)
    m_bits = [0] + list(range(2, count, 2)) + list(range(1, count, 2))
    if by_pairs:
        starts = jnp.stack(
            [(index[0] ^ jnp.int32(b)) * share for b in (*bits, *range(count), *m_bits)]
        )
    else:
        starts = jnp.zeros((3,), jnp.int32)
    full = pltpu.VMEM((DH, columns), BF16)
    tokens = pltpu.VMEM(fast_key.shape, BF16)
    grads = call(
        functools.partial(gradient_kernel, pieces, 1.0 / math.sqrt(rows * count)),
        [shape(weights[0].shape, BF16)] * pieces,
        (starts, fast_key, fast_value, token_rate, *weights),
        smem=(0,),
        scratch=(tokens, tokens, pltpu.VMEM(token_rate.shape, F32), full, full),
        copies=3 + 2 * pieces,
        cost=pl.CostEstimate(
            flops=12 * rows * DH * FH * heads,
            bytes_accessed=4 * DH * columns + 4 * rows * DH * heads,
            transcendentals=rows * FH * heads,
        ),
    )
    if by_pairs:
        terms = scattered(grads)
    else:
        terms = [
            lax.psum_scatter(
                grads[0].astype(F32), AXIS, scatter_dimension=0, tiled=True
            ).astype(BF16)
        ]
    state = (pltpu.VMEM(m_in.shape, F32), pltpu.VMEM(m_out.shape, F32))
    new_m_in, new_m_out, packed_m = call(
        functools.partial(momentum_kernel, len(terms)),
        [shape(m_in.shape, F32), shape(m_out.shape, F32), shape(part, BF16)],
        (*terms, m_in, m_out),
        scratch=(pltpu.VMEM(part, BF16),) * len(terms) + state * 2 + (pltpu.VMEM(part, BF16),),
        copies=len(terms) + 5,
    )
    if by_pairs:
        momenta, m_order = gathered(packed_m)
        assert m_order == m_bits
    else:
        momenta = [lax.all_gather(packed_m, AXIS, axis=0, tiled=True)]
    momenta[-1], done = lax.optimization_barrier((momenta[-1], before_apply))
    fast_out, new_w_in, new_w_out = call(
        functools.partial(apply_kernel, pieces),
        [shape(fast_query.shape, BF16), shape(w_in.shape, F32), shape(w_out.shape, F32)],
        (starts, step_size, fast_query, *weights, *momenta, w_in, w_out, new_m_in, new_m_out),
        smem=(0, 1),
        scratch=(tokens, *state, *state, full, full, tokens),
        copies=2 * pieces + 8,
        cost=pl.CostEstimate(
            flops=6 * rows * DH * FH * heads,
            bytes_accessed=4 * DH * columns + 4 * rows * DH * heads,
            transcendentals=rows * FH * heads,
        ),
    )
    outs = (new_w_in, new_w_out, new_m_in, new_m_out)
    return (done, fast_out, *(jnp.swapaxes(a, 1, 2) for a in outs))


def body(
    attn_query,
    attn_key,
    attn_value,
    lookback,
    frame_start,
    fast_query,
    fast_key,
    fast_value,
    token_rate,
    w_in,
    w_out,
    momentum_in,
    momentum_out,
    step_size,
):
    index = lax.axis_index(AXIS).astype(jnp.int32)[None]
    attn_out = attend(index, attn_query, attn_key, attn_value, lookback, frame_start)
    return fast_layer(
        index,
        fast_query,
        fast_key,
        fast_value,
        token_rate,
        w_in,
        w_out,
        momentum_in,
        momentum_out,
        step_size,
        attn_out,
    )


def solution(mesh):
    tokens, weights = P(("groups", "ctx"), "head"), P("head", None, "ctx")
    state = P(("groups", "head"), None, "ctx")
    positions = P(("groups", "ctx"))
    return jax.shard_map(
        body,
        mesh=mesh,
        in_specs=(
            (tokens,) * 3 + (positions,) * 2 + (tokens,) * 4 + (weights,) * 2 + (state,) * 2
        )
        + (P("head"),),
        out_specs=(tokens,) * 2 + (state,) * 4,
        check_vma=False,
    )
```

```python
import functools
import math

import jax
import jax.numpy as jnp
from jax import lax
from jax.experimental import pallas as pl
from jax.experimental.pallas import tpu as pltpu
from jax.sharding import PartitionSpec as P


ATT_DIM = 128
DH = 512
FH = 320
WINDOW = 768
AXIS = "ctx"
GROUPS = "groups"
F32 = jnp.float32
BF16 = jnp.bfloat16
HBM, VMEM, SMEM = pltpu.MemorySpace.HBM, pltpu.MemorySpace.VMEM, pltpu.MemorySpace.SMEM
LIMIT = 20 << 20


def moved(value, steps, first):
    count = lax.axis_size(AXIS)
    return lax.ppermute(value, AXIS, [(i, i + steps) for i in range(first, count - steps)])


def swapped(value, bits):
    return lax.ppermute(value, AXIS, [(i, i ^ bits) for i in range(lax.axis_size(AXIS))])


def across(value, bits_of):
    groups, count = lax.axis_size(GROUPS), lax.axis_size(AXIS)
    pairs = []
    for group in range(groups):
        bits, flip = bits_of(group)
        for place in range(count):
            pairs.append((group * count + place, (group ^ flip) * count + (place ^ bits)))
    return lax.ppermute(value, (GROUPS, AXIS), pairs)


def call(kernel, out_shape, operands, places, out_places, scratch=(), copies=0, cost=None):
    return pl.pallas_call(
        kernel,
        out_shape=out_shape,
        in_specs=[pl.BlockSpec(memory_space=place) for place in places],
        out_specs=jax.tree.map(lambda place: pl.BlockSpec(memory_space=place), out_places),
        scratch_shapes=[*scratch, *([pltpu.SemaphoreType.DMA((copies,))] if copies else [])],
        compiler_params=pltpu.CompilerParams(vmem_limit_bytes=LIMIT),
        cost_estimate=cost,
    )(*operands)


class Copies:
    def __init__(self, sems):
        self.sems, self.used = sems, 0

    def make(self, source, target):
        copy = pltpu.make_async_copy(source, target, self.sems.at[self.used])
        self.used += 1
        return copy

    def start(self, source, target):
        copy = self.make(source, target)
        copy.start()
        return copy


def down(row, width):
    size = row.shape[1]
    column = jnp.broadcast_to(row.astype(F32), (size, size)).T
    if width % size == 0:
        whole = jnp.concatenate([column] * (width // size), axis=1)
    else:
        whole = jnp.broadcast_to(column[:, :1], (size, width))
    return whole.astype(row.dtype)


def column_blocks(value, reach):
    blocks = [value]
    for j in range(1, reach + 1):
        blocks.append(moved(blocks[-1], 2, 2 * (j - 1)))
    return blocks[1:]


def attention_kernel(reach, index_ref, low_ref, low_other_ref, q_ref, q_other_ref, *refs):
    keys_in, values_in = refs[: reach + 1], refs[reach + 1 : 2 * reach + 2]
    own_ref, own_stat_ref, other_ref, other_stat_ref, bias_ref = refs[2 * reach + 2 :]
    rows = q_ref.shape[0]
    keys = bias_ref.shape[1]
    place = lax.broadcasted_iota(jnp.int32, (rows, keys), 1)
    key_pos = 2 * (place - reach * rows) - lax.rem(place, rows)
    query_pos = lax.broadcasted_iota(jnp.int32, (rows, keys), 0)
    shift = jnp.where(index_ref[0] % 2 == 0, rows, -rows)
    seen = (key_pos >= down(low_ref[...], keys)) & (key_pos <= query_pos)
    bias_ref[:rows] = jnp.where(seen, 0.0, -1e30).astype(F32)
    key_pos -= shift
    seen = (key_pos >= down(low_other_ref[...], keys)) & (key_pos <= query_pos)
    bias_ref[rows:] = jnp.where(seen, 0.0, -1e30).astype(F32)
    lane = lax.broadcasted_iota(jnp.int32, (2 * rows, own_stat_ref.shape[1]), 1)
    stat = jnp.zeros(lane.shape, F32)
    for head in range(q_ref.shape[1] // ATT_DIM):
        cols = slice(head * ATT_DIM, (head + 1) * ATT_DIM)
        queries = jnp.concatenate([q_ref[:, cols], q_other_ref[:, cols]], axis=0)
        key_all = jnp.concatenate([k[:, cols] for k in reversed(keys_in)], axis=0)
        value_all = jnp.concatenate([v[:, cols] for v in reversed(values_in)], axis=0)
        scores = lax.dot_general(
            queries, key_all, (((1,), (1,)), ((), ())), preferred_element_type=F32
        )
        scores = scores * (1.0 / math.sqrt(ATT_DIM)) + bias_ref[...]
        peak = jnp.max(scores, axis=1, keepdims=True)
        weights = jnp.exp(scores - peak)
        total = jnp.sum(weights, axis=1, keepdims=True)
        result = jnp.dot(weights.astype(BF16), value_all, preferred_element_type=F32) / total
        own_ref[:, cols] = result[:rows]
        other_ref[:, cols] = result[rows:].astype(BF16)
        stat = jnp.where(lane == head, peak + jnp.log(total), stat)
    own_stat_ref[...] = stat[:rows]
    other_stat_ref[...] = stat[rows:]


def combine_kernel(own_ref, own_stat_ref, other_ref, other_stat_ref, o_ref):
    own_stat, other_stat = own_stat_ref[...], other_stat_ref[...]
    peak = jnp.maximum(own_stat, other_stat)
    own_part, other_part = jnp.exp(own_stat - peak), jnp.exp(other_stat - peak)
    total = own_part + other_part
    own_part, other_part = own_part / total, other_part / total
    for head in range(o_ref.shape[1] // ATT_DIM):
        cols = slice(head * ATT_DIM, (head + 1) * ATT_DIM)
        part = slice(head, head + 1)
        result = own_ref[:, cols] * own_part[:, part]
        o_ref[:, cols] = (result + other_ref[:, cols].astype(F32) * other_part[:, part]).astype(BF16)


def attend_partly(ids, low, attn_query, attn_key, attn_value):
    rows, width = attn_query.shape
    reach = (WINDOW + rows - 2) // rows
    reach = (reach + 1) // 2
    low_other = swapped(low, 1)
    query_other = swapped(attn_query, 1)
    key_blocks = [attn_key, *column_blocks(attn_key, reach)]
    value_blocks = [attn_value, *column_blocks(attn_value, reach)]
    keys = (reach + 1) * rows
    lanes = -(-(width // ATT_DIM) // 128) * 128
    shape = jax.ShapeDtypeStruct
    out = call(
        functools.partial(attention_kernel, reach),
        [
            shape((rows, width), F32),
            shape((rows, lanes), F32),
            shape((rows, width), BF16),
            shape((rows, lanes), F32),
        ],
        (ids, low, low_other, attn_query, query_other, *key_blocks, *value_blocks),
        (SMEM,) + (VMEM,) * (6 + 2 * reach),
        [VMEM] * 4,
        scratch=(pltpu.VMEM((2 * rows, keys), F32),),
        cost=pl.CostEstimate(
            flops=8 * rows * keys * width,
            bytes_accessed=4 * (keys + 3 * rows) * width,
            transcendentals=2 * rows * keys * width // ATT_DIM,
        ),
    )
    return out[:2], out[2:]


def attend_rest(own, other):
    back = (swapped(other[0], 1), swapped(other[1], 1))
    return call(
        combine_kernel, jax.ShapeDtypeStruct(other[0].shape, BF16), (*own, *back), (VMEM,) * 4, VMEM
    )


def in_cols(head):
    return slice(head * 2 * FH, (head + 1) * 2 * FH)


def out_cols(heads, head):
    return slice((2 * heads + head) * FH, (2 * heads + head + 1) * FH)


def pack_kernel(ids_ref, in_ref, out_ref, lookback_ref, frame_ref, packed, low_ref):
    heads = in_ref.shape[0]
    for head in range(heads):
        packed[:, in_cols(head)] = in_ref[head].astype(BF16)
        packed[:, out_cols(heads, head)] = out_ref[head].astype(BF16)
    rows = lookback_ref.shape[1]
    query_pos = lax.broadcasted_iota(jnp.int32, (1, rows), 1)
    low_ref[...] = jnp.maximum(
        frame_ref[...] - ids_ref[0] * rows, query_pos - lookback_ref[...] + 1
    )


def share_of(ids_ref, bits, rows):
    if isinstance(bits, tuple):
        other, low = bits
        bits = (6 - 2 * ids_ref[1] if other else 4 + 2 * ids_ref[1]) + low
    return pl.ds(pl.multiple_of((ids_ref[0] ^ bits) * rows, rows), rows)


def add_kernel(own_ref, other_ref, sum_ref):
    sum_ref[...] = (own_ref[...].astype(F32) + other_ref[...].astype(F32)).astype(BF16)


def gradient_kernel(bits, rate_norm, ids_ref, key_ref, value_ref, rate_ref, *refs):
    count = len(bits)
    parts, grads = refs[:count], refs[count : 2 * count]
    whole_hbm, w_ref, g_ref, sems = refs[2 * count :]
    rows = parts[0].shape[0]
    heads = rate_ref.shape[0]
    for which, part in zip(bits, parts, strict=True):
        w_ref[share_of(ids_ref, which, rows)] = part[...]
    keep = Copies(sems).start(w_ref, whole_hbm)
    for head in range(heads):
        cols = slice(head * DH, (head + 1) * DH)
        keys = key_ref[:, cols]
        mixed = jnp.dot(keys, w_ref[:, in_cols(head)], preferred_element_type=F32)
        gate, up = mixed[:, :FH], mixed[:, FH:]
        sig = jax.nn.sigmoid(gate)
        silu = gate * sig
        hidden = (silu * up).astype(BF16)
        rate = -(down(rate_ref[head : head + 1], DH) * rate_norm)
        out_grad = (rate * value_ref[:, cols].astype(F32)).astype(BF16)
        grad_out = lax.dot_general(
            out_grad, hidden, (((0,), (0,)), ((), ())), preferred_element_type=F32
        )
        g_ref[:, out_cols(heads, head)] = grad_out.astype(BF16)
        hid_grad = jnp.dot(out_grad, w_ref[:, out_cols(heads, head)], preferred_element_type=F32)
        gate_grad = hid_grad * up * (sig * (1.0 + gate * (1.0 - sig)))
        mix_grad = jnp.concatenate([gate_grad, hid_grad * silu], axis=1).astype(BF16)
        grad_in = lax.dot_general(
            keys, mix_grad, (((0,), (0,)), ((), ())), preferred_element_type=F32
        )
        g_ref[:, in_cols(head)] = grad_in.astype(BF16)
    for place, grad in enumerate(grads):
        grad[...] = g_ref[share_of(ids_ref, place, rows)]
    keep.wait()


def momentum_kernel(count, *refs):
    parts, (old_in, old_out, fresh_ref, packed) = refs[:count], refs[count:]
    heads = old_in.shape[0]
    for head in range(heads):
        for old, cols in ((old_in, in_cols(head)), (old_out, out_cols(heads, head))):
            grad = parts[0][:, cols].astype(F32)
            for part in parts[1:]:
                grad = grad + part[:, cols].astype(F32)
            fresh = 0.9 * old[head] + grad
            fresh_ref[:, cols] = fresh
            packed[:, cols] = fresh.astype(BF16)


def apply_kernel(bits, ids_ref, step_ref, query_ref, w_ref, w_in, w_out, fresh_ref, *refs):
    count = len(bits)
    momenta, outs = refs[:count], refs[count : count + 5]
    fast_ref, new_in, new_out, new_m_in, new_m_out = outs
    m_ref = refs[count + 5]
    rows = momenta[0].shape[0]
    heads = w_in.shape[0]
    square = None
    for which, part in zip(bits, momenta, strict=True):
        m_ref[share_of(ids_ref, which, rows)] = part[...]
        value = part[...].astype(F32)
        term = jnp.sum(value * value, axis=0, keepdims=True)
        square = term if square is None else square + term
    norm = lax.rsqrt(square * (1.0 / DH) + 1e-06)
    for head in range(heads):
        cols = slice(head * DH, (head + 1) * DH)
        cols_in, cols_out = in_cols(head), out_cols(heads, head)
        scale_in = step_ref[head] * norm[:, cols_in]
        scale_out = step_ref[head] * norm[:, cols_out]
        mixed = jnp.dot(query_ref[:, cols], w_ref[:, cols_in], preferred_element_type=F32)
        mixed -= scale_in * jnp.dot(
            query_ref[:, cols], m_ref[:, cols_in], preferred_element_type=F32
        )
        gate, up = mixed[:, :FH], mixed[:, FH:]
        hidden = (gate * jax.nn.sigmoid(gate) * up).astype(BF16)
        fresh = w_ref[:, cols_out].astype(F32) - m_ref[:, cols_out].astype(F32) * scale_out
        fast_ref[:, cols] = lax.dot_general(
            hidden,
            fresh.astype(BF16),
            (((1,), (1,)), ((), ())),
            preferred_element_type=F32,
        ).astype(BF16)
        new_m_in[head] = fresh_ref[:, cols_in]
        new_m_out[head] = fresh_ref[:, cols_out]
        new_in[head] = w_in[head] - fresh_ref[:, cols_in] * scale_in
        new_out[head] = w_out[head] - fresh_ref[:, cols_out] * scale_out


def gathered(part):
    count = lax.axis_size(AXIS)
    parts = {0: part}
    for bits in range(2, count, 2):
        parts[bits] = swapped(part, bits)
    for bits in range(0, count, 2):
        parts[bits + 1] = swapped(parts[bits], 1)
    return list(parts.values()), list(parts)


def gathered_twin(part):
    near = swapped(part, 2)
    far = across(part, lambda g: (4 + 2 * (g % 2), 0))
    own_x = swapped(part, 1)
    near_x = swapped(near, 1)
    far_y = across(far, lambda g: (0, 1))
    far_x = swapped(far, 1)
    far_xy = across(far_x, lambda g: (0, 1))
    parts = [part, near, own_x, near_x, far, far_y, far_x, far_xy]
    return parts, [0, 2, 1, 3, (0, 0), (1, 0), (0, 1), (1, 1)]


def scattered(parts):
    count = len(parts)
    terms = []
    for bits in range(count - 2, -1, -2):
        other = swapped(parts[bits + 1], 1)
        pair = call(
            add_kernel,
            jax.ShapeDtypeStruct(other.shape, BF16),
            (parts[bits], other),
            (VMEM, VMEM),
            VMEM,
        )
        terms.append(swapped(pair, bits) if bits else pair)
    return terms


def layer(
    attn_query,
    attn_key,
    attn_value,
    lookback,
    frame_start,
    fast_query,
    fast_key,
    fast_value,
    token_rate,
    w_in,
    w_out,
    m_in,
    m_out,
    step_size,
):
    count = lax.axis_size(AXIS)
    rows = fast_key.shape[0]
    heads, _, share = w_in.shape
    columns = 3 * heads * FH
    by_pairs = count & (count - 1) == 0 and count > 1 and share % 16 == 0
    shape = jax.ShapeDtypeStruct
    w_in, w_out, m_in, m_out = (jnp.swapaxes(a, 1, 2) for a in (w_in, w_out, m_in, m_out))
    part = (share, columns)
    ids = jnp.stack([lax.axis_index(AXIS), lax.axis_index(GROUPS) % 2]).astype(jnp.int32)
    packed, low = call(
        pack_kernel,
        [shape(part, BF16), shape((1, rows), jnp.int32)],
        (ids, w_in, w_out, lookback[None], frame_start[None]),
        (SMEM,) + (VMEM,) * 4,
        [VMEM, VMEM],
    )
    attention = attend_partly(ids, low, attn_query, attn_key, attn_value)
    if not by_pairs:
        weights, bits = [lax.all_gather(packed, AXIS, axis=0, tiled=True)], [0]
        ids = ids * 0
    elif count == 8 and lax.axis_size(GROUPS) % 2 == 0:
        weights, bits = gathered_twin(packed)
    else:
        weights, bits = gathered(packed)
    pieces = len(weights)
    full = pltpu.VMEM((DH, columns), BF16)
    *grads, whole = call(
        functools.partial(gradient_kernel, bits, 1.0 / math.sqrt(rows * count)),
        [shape(weights[0].shape, BF16)] * pieces + [shape((DH, columns), BF16)],
        (ids, fast_key, fast_value, token_rate.T, *weights),
        (SMEM,) + (VMEM,) * (3 + pieces),
        [VMEM] * pieces + [HBM],
        scratch=(full, full),
        copies=1,
        cost=pl.CostEstimate(
            flops=12 * rows * DH * FH * heads,
            bytes_accessed=4 * DH * columns + 4 * rows * DH * heads,
            transcendentals=rows * FH * heads,
        ),
    )
    if by_pairs:
        terms = scattered(grads)
    else:
        terms = [
            lax.psum_scatter(
                grads[0].astype(F32), AXIS, scatter_dimension=0, tiled=True
            ).astype(BF16)
        ]
    terms[-1], attention = lax.optimization_barrier((terms[-1], attention))
    fresh, packed_m = call(
        functools.partial(momentum_kernel, len(terms)),
        [shape(part, F32), shape(part, BF16)],
        (*terms, m_in, m_out),
        (VMEM,) * (len(terms) + 2),
        [VMEM, VMEM],
    )
    if by_pairs:
        momenta, bits = gathered(packed_m)
    else:
        momenta, bits = [lax.all_gather(packed_m, AXIS, axis=0, tiled=True)], [0]
    momenta[-1], done = lax.optimization_barrier((momenta[-1], attend_rest(*attention)))
    fast_out, new_w_in, new_w_out, new_m_in, new_m_out = call(
        functools.partial(apply_kernel, bits),
        [shape(fast_query.shape, BF16)] + [shape(a.shape, F32) for a in (w_in, w_out, m_in, m_out)],
        (ids, step_size, fast_query, whole, w_in, w_out, fresh, *momenta),
        (SMEM, SMEM) + (VMEM,) * (5 + pieces),
        [VMEM] * 5,
        scratch=(full,),
        cost=pl.CostEstimate(
            flops=9 * rows * DH * FH * heads,
            bytes_accessed=4 * DH * columns + 4 * rows * DH * heads,
            transcendentals=rows * FH * heads,
        ),
    )
    outs = (new_w_in, new_w_out, new_m_in, new_m_out)
    return (done, fast_out, *(jnp.swapaxes(a, 1, 2) for a in outs))


def solution(mesh):
    tokens, weights = P(("groups", "ctx"), "head"), P("head", None, "ctx")
    state = P(("groups", "head"), None, "ctx")
    positions = P(("groups", "ctx"))
    return jax.shard_map(
        layer,
        mesh=mesh,
        in_specs=(
            (tokens,) * 3 + (positions,) * 2 + (tokens,) * 4 + (weights,) * 2 + (state,) * 2
        )
        + (P("head"),),
        out_specs=(tokens,) * 2 + (state,) * 4,
        check_vma=False,
    )
```
